512 devices in a mesh: dp: 16 (over x_lo, y), tensor: 32 (over z, x_hi, core).
Axes of the slice: x: 4 (x_hi: 2, x_lo: 2; x = x_hi * 2 + x_lo), y: 8, z: 8, core: 2. Of those that a mesh axis runs over, the one named last changes fastest.
Arguments:
- tokens_in: bfloat16 [8192, 128, 128], P('dp', 'tensor'), may hold values from -6 to 6
- right_one: bfloat16 [128, 128, 128], P('tensor'), may hold values from -0.5 to 0.5
- left_one: bfloat16 [128, 128, 128], P('tensor'), may hold values from -0.5 to 0.5
- right_two: bfloat16 [128, 128, 128], P('tensor'), may hold values from -0.5 to 0.5
- left_two: bfloat16 [128, 128, 128], P('tensor'), may hold values from -0.5 to 0.5
- out_grad: bfloat16 [8192, 128, 128], P('dp', 'tensor'), may hold values from -6 to 6
Outputs:
- layer_out: bfloat16 [8192, 128, 128], P('dp', 'tensor')
- input_grad: bfloat16 [8192, 128, 128], P('dp', 'tensor')
- grad_right_one: float32 [128, 128, 128], P('tensor', 'dp')
- grad_left_one: float32 [128, 128, 128], P('tensor', 'dp')
- grad_right_two: float32 [128, 128, 128], P('tensor', 'dp')
- grad_left_two: float32 [128, 128, 128], P('tensor', 'dp')
The draws below stay inside these ranges and needn't reach their ends.
All inputs are finite; a program needn't handle non-finite values.
Results may differ from the reference program's by a relative error of at most 0.0067.
Values may be sent and summed in bfloat16 or wider, within the bound.
No kernel may reach another device: no remote copies, remote signals or barrier semaphores. Data moves between devices by JAX's collectives and lax.ppermute only.
A program may use at most 64 MiB of HBM per device.

```python
import math
import jax
import jax.numpy as jnp
from jax import lax

BS = 128
NBLK = 128
TOKENS = 8192


def block_scale(own_key, shape, shards, least, largest):
    gain = 1.0
    for dim, parts in shards:
        steps = jax.random.uniform(jax.random.fold_in(jax.random.fold_in(own_key, 6), dim), (parts,), jnp.float32, least / len(shards), largest / len(shards))
        gain = gain * jnp.repeat(jnp.exp(steps), shape[dim] // parts).reshape((-1,) + (1,) * (len(shape) - 1 - dim))
    return gain


def bell_draw(rng, dims, spread, bound, split=(), kind=jnp.bfloat16):
    array = jax.random.normal(rng, dims, jnp.float32) * spread
    if len(split) > 0:
        array = block_scale(rng, dims, split, -0.22, 0.18) * array
    return jnp.clip(array, min=-bound, max=bound).astype(kind)


def setup_inputs(seed: int = 0) -> dict:
    key_list = jax.random.split(jax.random.key(seed), 7)
    return {
        "tokens_in": bell_draw(key_list[0], (TOKENS, NBLK, BS), 1.0, 6.0, ((0, 16), (1, 32))),
        "right_one": bell_draw(key_list[1], (NBLK, BS, BS), BS ** -0.5, 0.5, ((0, 32),)),
        "left_one": bell_draw(key_list[2], (NBLK, BS, BS), BS ** -0.5, 0.5, ((0, 32),)),
        "right_two": bell_draw(key_list[3], (NBLK, BS, BS), BS ** -0.5, 0.5, ((0, 32),)),
        "left_two": bell_draw(key_list[4], (NBLK, BS, BS), BS ** -0.5, 0.5, ((0, 32),)),
        "out_grad": bell_draw(key_list[5], (TOKENS, NBLK, BS), 1.0, 6.0, ((0, 16), (1, 32))),
    }


def gelu_value(z):
    return 0.5 * z * (1.0 + lax.erf(z / math.sqrt(2.0)))

def gelu_slope(z):
    return 0.5 * (1.0 + lax.erf(z / math.sqrt(2.0))) + z * jnp.exp(-0.5 * z * z) / math.sqrt(2.0 * math.pi)

def blockmul(a, w):
    return jnp.einsum('tpq,pqr->tpr', a.astype(jnp.float32), w.astype(jnp.float32))

def transpose_blocks(a):
    return jnp.swapaxes(a, 1, 2)

def one_block(tokens_in, out_grad, right_one, left_one, right_two, left_two):
    bf = jnp.bfloat16
    f32 = jnp.float32
    u1 = blockmul(tokens_in, right_one).astype(bf)
    v1 = transpose_blocks(u1)
    a1 = blockmul(v1, left_one).astype(bf)
    z1 = transpose_blocks(a1)
    hidden = gelu_value(z1.astype(f32)).astype(bf)
    u2 = blockmul(hidden, right_two).astype(bf)
    v2 = transpose_blocks(u2)
    w2 = blockmul(v2, left_two).astype(bf)
    layer_out = (tokens_in.astype(f32) + transpose_blocks(w2).astype(f32)).astype(bf)
    g2 = transpose_blocks(out_grad).astype(f32)
    gl2 = jnp.einsum('tpq,tpr->pqr', v2.astype(f32), g2)
    dv2 = jnp.einsum('tpr,pqr->tpq', g2, left_two.astype(f32)).astype(bf)
    du2 = transpose_blocks(dv2).astype(f32)
    gr2 = jnp.einsum('tpq,tpr->pqr', hidden.astype(f32), du2)
    dh = jnp.einsum('tpr,pqr->tpq', du2, right_two.astype(f32))
    dz1 = (dh * gelu_slope(z1.astype(f32))).astype(bf)
    da1 = transpose_blocks(dz1).astype(f32)
    gl1 = jnp.einsum('tpq,tpr->pqr', v1.astype(f32), da1)
    dv1 = jnp.einsum('tpr,pqr->tpq', da1, left_one.astype(f32)).astype(bf)
    du1 = transpose_blocks(dv1).astype(f32)
    gr1 = jnp.einsum('tpq,tpr->pqr', tokens_in.astype(f32), du1)
    input_grad = (out_grad.astype(f32) + jnp.einsum('tpr,pqr->tpq', du1, right_one.astype(f32))).astype(bf)
    return (layer_out, input_grad, gr1, gl1, gr2, gl2)

def reference(tokens_in, right_one, left_one, right_two, left_two, out_grad):
    rows = math.gcd(TOKENS, 2048)
    count = TOKENS // rows
    xs = tokens_in.reshape(count, rows, NBLK, BS)
    gs = out_grad.reshape(count, rows, NBLK, BS)
    zero = jnp.zeros((NBLK, BS, BS), jnp.float32)

    def step(carry, pair):
        res = one_block(pair[0], pair[1], right_one, left_one, right_two, left_two)
        carry = (carry[0] + res[2], carry[1] + res[3], carry[2] + res[4], carry[3] + res[5])
        return (carry, (res[0], res[1]))
    grads, outs = lax.scan(step, (zero, zero, zero, zero), (xs, gs))
    layer_out = outs[0].reshape(TOKENS, NBLK, BS)
    input_grad = outs[1].reshape(TOKENS, NBLK, BS)
    return (layer_out, input_grad, grads[0], grads[1], grads[2], grads[3])
```

```python
import math

import jax
import jax.numpy as jnp
from jax import lax
from jax.experimental import pallas as pl
from jax.experimental.pallas import tpu as pltpu
from jax.sharding import PartitionSpec as P

BF = jnp.bfloat16
F32 = jnp.float32


def in_to_flat(r):
    return (r & 3) * 128 + (r >> 2)


def flat_to_in(r):
    return (r & 127) * 4 + (r >> 7)


def out_to_flat(r):
    return ((r >> 2) & 3) * 128 + (r >> 4) * 4 + (r & 3)


def flat_to_out(r):
    return ((r & 127) >> 2) * 16 + (r >> 7) * 4 + (r & 3)


def one_hot(col_of_row, cols=512):
    row = lax.broadcasted_iota(jnp.int32, (512, 128), 0)
    col = lax.broadcasted_iota(jnp.int32, (512, 128), 1)
    at = col_of_row(row)
    parts = [jnp.where(at == col + j, 1.0, 0.0).astype(BF) for j in range(0, cols, 128)]
    return jnp.concatenate(parts, axis=1)


def dot(a, b, dims):
    return lax.dot_general(a, b, (dims, ((), ())), preferred_element_type=F32)


def nn(a, b):
    return dot(a, b, ((1,), (0,)))


def nt(a, b):
    return dot(a, b, ((1,), (1,)))


def tn(a, b):
    return dot(a, b, ((0,), (0,)))


def put_rows(ref, first, value):
    ref[:, first : first + 16, :] = value.astype(BF).reshape(32, 16, 512)


def get_rows(ref, first):
    return ref[:, first : first + 16, :].reshape(512, 512)


def by_block(ref):
    return [ref[pl.ds(b, 512, stride=4), :].astype(BF) for b in range(4)]


def right_one_out(r1_ref):
    spread = one_hot(out_to_flat)
    cols = [nt(spread[:, 128 * b : 128 * b + 128], r1_ref[b]).astype(BF) for b in range(4)]
    return jnp.concatenate(cols, axis=1)


def first_kernel(x_ref, g_ref, r1_ref, out_ref, xs_ref, gs_ref):
    xs_ref[...] = x_ref[...].astype(F32)
    gs_ref[...] = g_ref[...].astype(F32)
    x = jnp.concatenate(by_block(xs_ref), axis=1)
    put_rows(out_ref, 0, nt(right_one_out(r1_ref), x))
    g = jnp.concatenate(by_block(gs_ref), axis=1)
    put_rows(out_ref, 16, nt(one_hot(in_to_flat), g))


def weights_kernel(l1_ref, r2_ref, l2_ref, *out_refs):
    spread_in = one_hot(in_to_flat)
    spread_out = one_hot(out_to_flat)
    for n, w_ref in enumerate((l1_ref, r2_ref, l2_ref)):
        parts = [nn(spread_in[:, 128 * b : 128 * b + 128], w_ref[b]).astype(BF) for b in range(4)]
        wide = jnp.concatenate(parts, axis=1)
        out_refs[2 * n][...] = nt(spread_out, wide).astype(BF)
        out_refs[2 * n + 1][...] = nt(wide, spread_out).astype(BF)


def mix_kernel(got_ref, fwd_ref, bwd_ref, out_ref):
    put_rows(out_ref, 0, nn(fwd_ref[...], get_rows(got_ref, 0)))
    put_rows(out_ref, 16, nn(bwd_ref[...], get_rows(got_ref, 16)))


def gelu_kernel(got_ref, fwd_ref, bwd_ref, out_ref, h_ref):
    z = get_rows(got_ref, 0).astype(F32)
    cdf = 0.5 * (1.0 + lax.erf(z * (1.0 / math.sqrt(2.0))))
    h = (z * cdf).astype(BF)
    h_ref[...] = h
    put_rows(out_ref, 0, nn(fwd_ref[...], h))
    slope = cdf + z * jnp.exp(-0.5 * z * z) * (1.0 / math.sqrt(2.0 * math.pi))
    put_rows(out_ref, 16, nn(bwd_ref[...], get_rows(got_ref, 16)) * slope)


def grad_of(fwd, bwd, out_ref):
    a = nn(one_hot(flat_to_in), fwd).astype(BF)
    b = nn(one_hot(flat_to_out), bwd).astype(BF)
    for m in range(4):
        at = slice(128 * m, 128 * m + 128)
        out_ref[m] = nt(a[at], b[at]).astype(BF)


def hidden_grad_kernel(h_ref, got_ref, out_ref):
    grad_of(h_ref[...], get_rows(got_ref, 16), out_ref)


def left_grads_kernel(one_ref, three_ref, l1_ref, l2_ref):
    grad_of(get_rows(one_ref, 0), get_rows(three_ref, 16), l1_ref)
    grad_of(get_rows(three_ref, 0), get_rows(one_ref, 16), l2_ref)


def right_grad_kernel(got_ref, x_ref, l1_ref, r2_ref, l2_ref, out_ref, xs_ref):
    xs_ref[...] = x_ref[...].astype(F32)
    d = nn(one_hot(flat_to_out), get_rows(got_ref, 16)).astype(BF)
    for b, x in enumerate(by_block(xs_ref)):
        g = jnp.transpose(nn(d[128 * b : 128 * b + 128], x))
        out_ref[:, b, :, :] = g.reshape(16, 8, 128).astype(BF)
    for n, ref in enumerate((l1_ref, r2_ref, l2_ref)):
        for b in range(4):
            g = ref[b].astype(F32).reshape(16, 8, 128)
            out_ref[:, 4 * n + 4 + b, :, :] = g.astype(BF)


def last_kernel(got_ref, x_ref, g_ref, r1_ref, out_ref, in_ref, s_ref):
    mixed = tn(get_rows(got_ref, 0), one_hot(in_to_flat))
    for b in range(4):
        s_ref[pl.ds(b, 512, stride=4), :] = mixed[:, 128 * b : 128 * b + 128]
    out_ref[...] = (x_ref[...].astype(F32) + s_ref[...]).astype(BF)
    back = tn(get_rows(got_ref, 16), right_one_out(r1_ref))
    for b in range(4):
        s_ref[pl.ds(b, 512, stride=4), :] = back[:, 128 * b : 128 * b + 128]
    in_ref[...] = (g_ref[...].astype(F32) + s_ref[...]).astype(BF)


def sum_kernel(got_ref, r1_ref, l1_ref, r2_ref, l2_ref):
    for n, ref in enumerate((r1_ref, l1_ref, r2_ref, l2_ref)):
        total = got_ref[0, 4 * n : 4 * n + 4].astype(F32)
        for k in range(1, 16):
            total = total + got_ref[k, 4 * n : 4 * n + 4].astype(F32)
        ref[...] = total


def call(kernel, shapes, *args, scratch=()):
    outs = [jax.ShapeDtypeStruct(s, d) for s, d in shapes]
    with jax.named_scope(kernel.__name__):
        return pl.pallas_call(
            kernel,
            out_shape=outs,
            scratch_shapes=[pltpu.VMEM(s, F32) for s in scratch],
            name=kernel.__name__,
        )(*args)


def swap(x, axis):
    return lax.all_to_all(x, axis, 0, 0, tiled=True)


def on_device(tokens_in, right_one, left_one, right_two, left_two, out_grad):
    x = tokens_in.reshape(2048, 128)
    g = out_grad.reshape(2048, 128)
    chunk = ((32, 32, 512), BF)
    square = ((512, 512), BF)
    grad = ((4, 128, 128), BF)
    rows = (2048, 128)
    (send,) = call(first_kernel, [chunk], x, g, right_one, scratch=(rows, rows))
    one = swap(send, "tensor")
    l1t, l1n, r2t, r2n, l2t, l2n = call(weights_kernel, [square] * 6, left_one, right_two, left_two)
    (send,) = call(mix_kernel, [chunk], one, l1t, l2n)
    two = swap(send, "tensor")
    send, h = call(gelu_kernel, [chunk, square], two, r2t, r2n)
    three = swap(send, "tensor")
    (gr2,) = call(hidden_grad_kernel, [grad], h, two)
    (send,) = call(mix_kernel, [chunk], three, l2t, l1n)
    four = swap(send, "tensor")
    gl1, gl2 = call(left_grads_kernel, [grad] * 2, one, three)
    (send,) = call(right_grad_kernel, [((16, 16, 8, 128), BF)], four, x, gl1, gr2, gl2, scratch=(rows,))
    sums = swap(send, "dp")
    layer_out, input_grad = call(last_kernel, [(rows, BF)] * 2, four, x, g, right_one, scratch=(rows,))
    grads = call(sum_kernel, [((4, 8, 128), F32)] * 4, sums)
    return (layer_out.reshape(512, 4, 128), input_grad.reshape(512, 4, 128), *grads)


def solution(mesh):
    placed = (
        P("dp", "tensor", None),
        P("tensor", None, None),
        P("tensor", None, None),
        P("tensor", None, None),
        P("tensor", None, None),
        P("dp", "tensor", None),
    )
    return jax.shard_map(
        on_device,
        mesh=mesh,
        in_specs=placed,
        out_specs=(
            P("dp", "tensor", None),
            P("dp", "tensor", None),
            P("tensor", "dp", None),
            P("tensor", "dp", None),
            P("tensor", "dp", None),
            P("tensor", "dp", None),
        ),
        check_vma=False,
    )
```

```python
import math

import jax
import jax.numpy as jnp
from jax import lax
from jax.experimental import pallas as pl
from jax.experimental.pallas import tpu as pltpu
from jax.sharding import PartitionSpec as P

BF = jnp.bfloat16
F32 = jnp.float32


def in_to_flat(r):
    return (r & 3) * 128 + (r >> 2)


def flat_to_in(r):
    return (r & 127) * 4 + (r >> 7)


def out_to_flat(r):
    return ((r >> 2) & 3) * 128 + (r >> 4) * 4 + (r & 3)


def flat_to_out(r):
    return ((r & 127) >> 2) * 16 + (r >> 7) * 4 + (r & 3)


def one_hot(col_of_row, cols=512):
    row = lax.broadcasted_iota(jnp.int32, (512, 128), 0)
    col = lax.broadcasted_iota(jnp.int32, (512, 128), 1)
    at = col_of_row(row)
    parts = [jnp.where(at == col + j, 1.0, 0.0).astype(BF) for j in range(0, cols, 128)]
    return jnp.concatenate(parts, axis=1)


def dot(a, b, dims):
    return lax.dot_general(a, b, (dims, ((), ())), preferred_element_type=F32)


def nn(a, b):
    return dot(a, b, ((1,), (0,)))


def nt(a, b):
    return dot(a, b, ((1,), (1,)))


def tn(a, b):
    return dot(a, b, ((0,), (0,)))


def put_rows(ref, first, value):
    ref[:, first : first + 16, :] = value.astype(BF).reshape(32, 16, 512)


def get_rows(ref, first):
    return ref[:, first : first + 16, :].reshape(512, 512)


def by_block(ref):
    return [ref[pl.ds(b, 512, stride=4), :].astype(BF) for b in range(4)]


def right_one_out(r1_ref):
    spread = one_hot(out_to_flat)
    cols = [nt(spread[:, 128 * b : 128 * b + 128], r1_ref[b]).astype(BF) for b in range(4)]
    return jnp.concatenate(cols, axis=1)


def fetch(pairs, sems):
    copies = [pltpu.make_async_copy(src, dst, sems.at[n]) for n, (src, dst) in enumerate(pairs)]
    for copy in copies:
        copy.start()
    return copies


def first_kernel(x_hbm, g_hbm, r1_hbm, out_ref, xs_ref, gs_ref, x_ref, g_ref, r1_ref, sems):
    r1_in, x_in, g_in = fetch(((r1_hbm, r1_ref), (x_hbm, x_ref), (g_hbm, g_ref)), sems)
    order = one_hot(in_to_flat)
    r1_in.wait()
    wide = right_one_out(r1_ref)
    x_in.wait()
    xs_ref[...] = x_ref[...].astype(F32)
    put_rows(out_ref, 0, nt(wide, jnp.concatenate(by_block(xs_ref), axis=1)))
    g_in.wait()
    gs_ref[...] = g_ref[...].astype(F32)
    put_rows(out_ref, 16, nt(order, jnp.concatenate(by_block(gs_ref), axis=1)))


def widen(w_ref, spread_in):
    parts = [nn(spread_in[:, 128 * b : 128 * b + 128], w_ref[b]).astype(BF) for b in range(4)]
    return jnp.concatenate(parts, axis=1)


def weights_kernel(fwd_ref, bwd_ref, fwd_out, bwd_out):
    spread_in = one_hot(in_to_flat)
    spread_out = one_hot(out_to_flat)
    fwd_out[...] = nt(spread_out, widen(fwd_ref, spread_in)).astype(BF)
    bwd_out[...] = nt(widen(bwd_ref, spread_in), spread_out).astype(BF)


def mix_kernel(got_ref, fwd_ref, bwd_ref, out_ref):
    put_rows(out_ref, 0, nn(fwd_ref[...], get_rows(got_ref, 0)))
    put_rows(out_ref, 16, nn(bwd_ref[...], get_rows(got_ref, 16)))


def gelu_kernel(got_ref, fwd_ref, bwd_ref, out_ref, h_ref):
    z = get_rows(got_ref, 0).astype(F32)
    cdf = 0.5 * (1.0 + lax.erf(z * (1.0 / math.sqrt(2.0))))
    h = (z * cdf).astype(BF)
    h_ref[...] = h
    put_rows(out_ref, 0, nn(fwd_ref[...], h))
    slope = cdf + z * jnp.exp(-0.5 * z * z) * (1.0 / math.sqrt(2.0 * math.pi))
    put_rows(out_ref, 16, nn(bwd_ref[...], get_rows(got_ref, 16)) * slope)


def grad_of(fwd, bwd, out_ref):
    a = nn(one_hot(flat_to_in), fwd).astype(BF)
    b = nn(one_hot(flat_to_out), bwd).astype(BF)
    for m in range(4):
        at = slice(128 * m, 128 * m + 128)
        out_ref[m] = nt(a[at], b[at]).astype(BF)


def hidden_grad_kernel(h_ref, got_hbm, out_ref, got_ref, sems):
    (got_in,) = fetch(((got_hbm, got_ref),), sems)
    got_in.wait()
    grad_of(h_ref[...], get_rows(got_ref, 16), out_ref)


def left_grads_kernel(one_hbm, three_hbm, l1_ref, l2_ref, one_ref, three_ref, sems):
    for copy in fetch(((one_hbm, one_ref), (three_hbm, three_ref)), sems):
        copy.wait()
    grad_of(get_rows(one_ref, 0), get_rows(three_ref, 16), l1_ref)
    grad_of(get_rows(three_ref, 0), get_rows(one_ref, 16), l2_ref)


def right_grad_kernel(got_ref, x_hbm, l1_ref, r2_ref, l2_ref, out_ref, xs_ref, x_ref, sems):
    (x_in,) = fetch(((x_hbm, x_ref),), sems)
    for n, ref in enumerate((l1_ref, r2_ref, l2_ref)):
        for b in range(4):
            g = ref[b].astype(F32).reshape(16, 8, 128)
            out_ref[:, 4 * n + 4 + b, :, :] = g.astype(BF)
    d = nn(one_hot(flat_to_out), get_rows(got_ref, 16)).astype(BF)
    x_in.wait()
    xs_ref[...] = x_ref[...].astype(F32)
    for b, x in enumerate(by_block(xs_ref)):
        g = jnp.transpose(nn(d[128 * b : 128 * b + 128], x))
        out_ref[:, b, :, :] = g.reshape(16, 8, 128).astype(BF)


def last_kernel(got_ref, x_ref, g_ref, r1_ref, out_ref, in_ref, s_ref):
    mixed = tn(get_rows(got_ref, 0), one_hot(in_to_flat))
    for b in range(4):
        s_ref[pl.ds(b, 512, stride=4), :] = mixed[:, 128 * b : 128 * b + 128]
    out_ref[...] = (x_ref[...].astype(F32) + s_ref[...]).astype(BF)
    back = tn(get_rows(got_ref, 16), right_one_out(r1_ref))
    for b in range(4):
        s_ref[pl.ds(b, 512, stride=4), :] = back[:, 128 * b : 128 * b + 128]
    in_ref[...] = (g_ref[...].astype(F32) + s_ref[...]).astype(BF)


def sum_kernel(got_ref, r1_ref, l1_ref, r2_ref, l2_ref):
    for n, ref in enumerate((r1_ref, l1_ref, r2_ref, l2_ref)):
        total = got_ref[0, 4 * n : 4 * n + 4].astype(F32)
        for k in range(1, 16):
            total = total + got_ref[k, 4 * n : 4 * n + 4].astype(F32)
        ref[...] = total


ROWS = (2048, 128)
WIDE_ROWS = pltpu.VMEM(ROWS, F32)
HALF_ROWS = pltpu.VMEM(ROWS, BF)
CHUNK = pltpu.VMEM((32, 32, 512), BF)


def call(kernel, shapes, *args, scratch=(), far=()):
    args = [pltpu.with_memory_space_constraint(a, pltpu.HBM) if n in far else a for n, a in enumerate(args)]
    outs = [jax.ShapeDtypeStruct(s, d) for s, d in shapes]
    specs = [pl.BlockSpec(memory_space=pltpu.HBM if n in far else pltpu.VMEM) for n in range(len(args))]
    with jax.named_scope(kernel.__name__):
        return pl.pallas_call(
            kernel,
            out_shape=outs,
            in_specs=specs,
            scratch_shapes=scratch,
            name=kernel.__name__,
            compiler_params=pltpu.CompilerParams(vmem_limit_bytes=16 << 20),
        )(*args)


def swap(x, axis):
    return lax.all_to_all(x, axis, 0, 0, tiled=True)


def after(first, *values):
    return lax.optimization_barrier((first, *values))[1:]


def on_device(tokens_in, right_one, left_one, right_two, left_two, out_grad):
    x = tokens_in.reshape(ROWS)
    g = out_grad.reshape(ROWS)
    chunk = ((32, 32, 512), BF)
    square = ((512, 512), BF)
    grad = ((4, 128, 128), BF)
    (send,) = call(
        first_kernel,
        [chunk],
        x,
        g,
        right_one,
        scratch=(
            WIDE_ROWS,
            WIDE_ROWS,
            HALF_ROWS,
            HALF_ROWS,
            pltpu.VMEM((4, 128, 128), BF),
            pltpu.SemaphoreType.DMA((3,)),
        ),
        far=(0, 1, 2),
    )
    one = swap(send, "tensor")
    fwd, bwd = call(weights_kernel, [square] * 2, *after(send, left_one, left_two))
    (send,) = call(mix_kernel, [chunk], one, fwd, bwd)
    (one,) = after(send, one)
    two = swap(send, "tensor")
    fwd, bwd = call(weights_kernel, [square] * 2, *after(send, right_two, right_two))
    send, h = call(gelu_kernel, [chunk, square], two, fwd, bwd)
    h, two = after(send, h, two)
    three = swap(send, "tensor")
    fwd, bwd = call(weights_kernel, [square] * 2, *after(send, left_two, left_one))
    (gr2,) = call(
        hidden_grad_kernel,
        [grad],
        h,
        two,
        scratch=(CHUNK, pltpu.SemaphoreType.DMA((1,))),
        far=(1,),
    )
    three, gr2 = lax.optimization_barrier((three, gr2))
    (send,) = call(mix_kernel, [chunk], three, fwd, bwd)
    (three,) = after(send, three)
    four = swap(send, "tensor")
    gl1, gl2 = call(
        left_grads_kernel,
        [grad] * 2,
        one,
        three,
        scratch=(CHUNK, CHUNK, pltpu.SemaphoreType.DMA((2,))),
        far=(0, 1),
    )
    (send,) = call(
        right_grad_kernel,
        [((16, 16, 8, 128), BF)],
        four,
        x,
        gl1,
        gr2,
        gl2,
        scratch=(WIDE_ROWS, HALF_ROWS, pltpu.SemaphoreType.DMA((1,))),
        far=(1,),
    )
    sums = swap(send, "dp")
    layer_out, input_grad = call(
        last_kernel, [(ROWS, BF)] * 2, four, x, g, right_one, scratch=(WIDE_ROWS,)
    )
    grads = call(sum_kernel, [((4, 8, 128), F32)] * 4, sums)
    return (layer_out.reshape(512, 4, 128), input_grad.reshape(512, 4, 128), *grads)


def solution(mesh):
    placed = (
        P("dp", "tensor", None),
        P("tensor", None, None),
        P("tensor", None, None),
        P("tensor", None, None),
        P("tensor", None, None),
        P("dp", "tensor", None),
    )
    return jax.shard_map(
        on_device,
        mesh=mesh,
        in_specs=placed,
        out_specs=(
            P("dp", "tensor", None),
            P("dp", "tensor", None),
            P("tensor", "dp", None),
            P("tensor", "dp", None),
            P("tensor", "dp", None),
            P("tensor", "dp", None),
        ),
        check_vma=False,
    )
```

```python
import math

import jax
import jax.numpy as jnp
from jax import lax
from jax.experimental import pallas as pl
from jax.experimental.pallas import tpu as pltpu
from jax.sharding import PartitionSpec as P


BF = jnp.bfloat16
F32 = jnp.float32


def in_to_flat(r):
    return (r & 3) * 128 + (r >> 2)


def flat_to_in(r):
    return (r & 127) * 4 + (r >> 7)


def out_to_flat(r):
    return ((r >> 2) & 3) * 128 + (r >> 4) * 4 + (r & 3)


def flat_to_out(r):
    return ((r & 127) >> 2) * 16 + (r >> 7) * 4 + (r & 3)


def one_hot(col_of_row, cols=512):
    row = lax.broadcasted_iota(jnp.int32, (512, 128), 0)
    col = lax.broadcasted_iota(jnp.int32, (512, 128), 1)
    at = col_of_row(row)
    parts = [jnp.where(at == col + j, 1.0, 0.0).astype(BF) for j in range(0, cols, 128)]
    return jnp.concatenate(parts, axis=1)


def dot(a, b, dims):
    return lax.dot_general(a, b, (dims, ((), ())), preferred_element_type=F32)


def nn(a, b):
    return dot(a, b, ((1,), (0,)))


def nt(a, b):
    return dot(a, b, ((1,), (1,)))


def tn(a, b):
    return dot(a, b, ((0,), (0,)))


def put_rows(ref, first, value):
    ref[:, first : first + 16, :] = value.astype(BF).reshape(32, 16, 512)


def get_rows(ref, first):
    return ref[:, first : first + 16, :].reshape(512, 512)


def by_block(ref):
    return [ref[pl.ds(b, 512, stride=4), :].astype(BF) for b in range(4)]


def right_one_out(r1_ref):
    spread = one_hot(out_to_flat)
    cols = [nt(spread[:, 128 * b : 128 * b + 128], r1_ref[b]).astype(BF) for b in range(4)]
    return jnp.concatenate(cols, axis=1)


def fetch(pairs, sems):
    copies = [pltpu.make_async_copy(src, dst, sems.at[n]) for n, (src, dst) in enumerate(pairs)]
    for copy in copies:
        copy.start()
    return copies


def first_kernel(x_hbm, g_hbm, r1_hbm, out_ref, xs_ref, gs_ref, x_ref, g_ref, r1_ref, sems):
    r1_in, x_in, g_in = fetch(((r1_hbm, r1_ref), (x_hbm, x_ref), (g_hbm, g_ref)), sems)
    order = one_hot(in_to_flat)
    r1_in.wait()
    wide = right_one_out(r1_ref)
    x_in.wait()
    xs_ref[...] = x_ref[...].astype(F32)
    put_rows(out_ref, 0, nt(wide, jnp.concatenate(by_block(xs_ref), axis=1)))
    g_in.wait()
    gs_ref[...] = g_ref[...].astype(F32)
    put_rows(out_ref, 16, nt(order, jnp.concatenate(by_block(gs_ref), axis=1)))


def widen(w_ref, spread_in):
    parts = [nn(spread_in[:, 128 * b : 128 * b + 128], w_ref[b]).astype(BF) for b in range(4)]
    return jnp.concatenate(parts, axis=1)


def weights_kernel(fwd_ref, bwd_ref, fwd_out, bwd_out):
    spread_in = one_hot(in_to_flat)
    spread_out = one_hot(out_to_flat)
    fwd_out[...] = nt(spread_out, widen(fwd_ref, spread_in)).astype(BF)
    bwd_out[...] = nt(widen(bwd_ref, spread_in), spread_out).astype(BF)


def mix_kernel(got_ref, fwd_ref, bwd_ref, out_ref):
    put_rows(out_ref, 0, nn(fwd_ref[...], get_rows(got_ref, 0)))
    put_rows(out_ref, 16, nn(bwd_ref[...], get_rows(got_ref, 16)))


def gelu_kernel(got_ref, fwd_ref, bwd_ref, out_ref, h_ref):
    z = get_rows(got_ref, 0).astype(F32)
    cdf = 0.5 * (1.0 + lax.erf(z * (1.0 / math.sqrt(2.0))))
    h = (z * cdf).astype(BF)
    h_ref[...] = h
    put_rows(out_ref, 0, nn(fwd_ref[...], h))
    slope = cdf + z * jnp.exp(-0.5 * z * z) * (1.0 / math.sqrt(2.0 * math.pi))
    put_rows(out_ref, 16, nn(bwd_ref[...], get_rows(got_ref, 16)) * slope)


def grad_of(fwd, bwd, out_ref, first):
    a = nn(one_hot(flat_to_in), fwd).astype(BF)
    b = nn(one_hot(flat_to_out), bwd).astype(BF)
    for m in range(4):
        at = slice(128 * m, 128 * m + 128)
        out_ref[:, first + m, :, :] = nt(a[at], b[at]).reshape(16, 8, 128).astype(BF)


def hidden_grad_kernel(h_ref, got_hbm, out_ref, got_ref, sems):
    (got_in,) = fetch(((got_hbm, got_ref),), sems)
    got_in.wait()
    grad_of(h_ref[...], get_rows(got_ref, 16), out_ref, 0)


def left_grads_kernel(one_hbm, three_hbm, out_ref, one_ref, three_ref, sems):
    for copy in fetch(((one_hbm, one_ref), (three_hbm, three_ref)), sems):
        copy.wait()
    grad_of(get_rows(one_ref, 0), get_rows(three_ref, 16), out_ref, 0)
    grad_of(get_rows(three_ref, 0), get_rows(one_ref, 16), out_ref, 4)


def right_grad_kernel(got_ref, x_hbm, out_ref, xs_ref, x_ref, sems):
    (x_in,) = fetch(((x_hbm, x_ref),), sems)
    d = nn(one_hot(flat_to_out), get_rows(got_ref, 16)).astype(BF)
    x_in.wait()
    xs_ref[...] = x_ref[...].astype(F32)
    for b, x in enumerate(by_block(xs_ref)):
        g = jnp.transpose(nn(d[128 * b : 128 * b + 128], x))
        out_ref[:, b, :, :] = g.reshape(16, 8, 128).astype(BF)


def last_kernel(got_ref, x_ref, g_ref, r1_ref, out_ref, in_ref, s_ref):
    mixed = tn(get_rows(got_ref, 0), one_hot(in_to_flat))
    for b in range(4):
        s_ref[pl.ds(b, 512, stride=4), :] = mixed[:, 128 * b : 128 * b + 128]
    out_ref[...] = (x_ref[...].astype(F32) + s_ref[...]).astype(BF)
    back = tn(get_rows(got_ref, 16), right_one_out(r1_ref))
    for b in range(4):
        s_ref[pl.ds(b, 512, stride=4), :] = back[:, 128 * b : 128 * b + 128]
    in_ref[...] = (g_ref[...].astype(F32) + s_ref[...]).astype(BF)


def sum_kernel(got_ref, out_ref):
    total = got_ref[0].astype(F32)
    for k in range(1, 16):
        total = total + got_ref[k].astype(F32)
    out_ref[...] = total


ROWS = (2048, 128)
WIDE_ROWS = pltpu.VMEM(ROWS, F32)
HALF_ROWS = pltpu.VMEM(ROWS, BF)
CHUNK = pltpu.VMEM((32, 32, 512), BF)


def call(kernel, shapes, *args, scratch=(), far=()):
    args = [pltpu.with_memory_space_constraint(a, pltpu.HBM) if n in far else a for n, a in enumerate(args)]
    outs = [jax.ShapeDtypeStruct(s, d) for s, d in shapes]
    specs = [pl.BlockSpec(memory_space=pltpu.HBM if n in far else pltpu.VMEM) for n in range(len(args))]
    return pl.pallas_call(
        kernel,
        out_shape=outs,
        in_specs=specs,
        scratch_shapes=scratch,
        compiler_params=pltpu.CompilerParams(vmem_limit_bytes=16 << 20),
    )(*args)


def swap(x, axis):
    return lax.all_to_all(x, axis, 0, 0, tiled=True)


def sent(x, mask):
    return lax.ppermute(x, "dp", [(i, i ^ mask) for i in range(16)])


def added(parts):
    me = lax.axis_index("dp")
    rest = parts.shape[1:]
    parts = parts.reshape(2, 4, 2, *rest)

    def near(who):
        at = (who >> 3, 0, who & 1) + (0,) * len(rest)
        return lax.dynamic_slice(parts, at, (1, 4, 1, *rest), allow_negative_indices=False).reshape(4, *rest)

    total = near(me).astype(F32)
    for mask in (8, 1, 9):
        total = total + sent(near(me ^ mask), mask).astype(F32)
    half = total.astype(BF)

    def far(who):
        return lax.dynamic_index_in_dim(half, (who >> 1) & 3, 0, False, allow_negative_indices=False)

    own = lax.dynamic_index_in_dim(total, (me >> 1) & 3, 0, False, allow_negative_indices=False)
    for mask in (2, 4, 6):
        own = own + sent(far(me ^ mask), mask).astype(F32)
    return own


def after(first, *values):
    return lax.optimization_barrier((first, *values))[1:]


def on_device(tokens_in, right_one, left_one, right_two, left_two, out_grad):
    x = tokens_in.reshape(ROWS)
    g = out_grad.reshape(ROWS)
    chunk = ((32, 32, 512), BF)
    square = ((512, 512), BF)
    (send,) = call(
        first_kernel,
        [chunk],
        x,
        g,
        right_one,
        scratch=(
            WIDE_ROWS,
            WIDE_ROWS,
            HALF_ROWS,
            HALF_ROWS,
            pltpu.VMEM((4, 128, 128), BF),
            pltpu.SemaphoreType.DMA((3,)),
        ),
        far=(0, 1, 2),
    )
    one = swap(send, "tensor")
    fwd, bwd = call(weights_kernel, [square] * 2, *after(send, left_one, left_two))
    (send,) = call(mix_kernel, [chunk], one, fwd, bwd)
    (one,) = after(send, one)
    two = swap(send, "tensor")
    fwd, bwd = call(weights_kernel, [square] * 2, *after(send, right_two, right_two))
    send, h = call(gelu_kernel, [chunk, square], two, fwd, bwd)
    h, two = after(send, h, two)
    three = swap(send, "tensor")
    fwd, bwd = call(weights_kernel, [square] * 2, *after(send, left_two, left_one))
    (gr2,) = call(
        hidden_grad_kernel,
        [((16, 4, 8, 128), BF)],
        h,
        two,
        scratch=(CHUNK, pltpu.SemaphoreType.DMA((1,))),
        far=(1,),
    )
    gr2 = added(gr2)
    three, gr2 = lax.optimization_barrier((three, gr2))
    (send,) = call(mix_kernel, [chunk], three, fwd, bwd)
    (three,) = after(send, three)
    four = swap(send, "tensor")
    (left,) = call(
        left_grads_kernel,
        [((16, 8, 8, 128), BF)],
        one,
        three,
        scratch=(CHUNK, CHUNK, pltpu.SemaphoreType.DMA((2,))),
        far=(0, 1),
    )
    left = added(left)
    four, left = lax.optimization_barrier((four, left))
    (send,) = call(
        right_grad_kernel,
        [((16, 4, 8, 128), BF)],
        four,
        x,
        scratch=(WIDE_ROWS, HALF_ROWS, pltpu.SemaphoreType.DMA((1,))),
        far=(1,),
    )
    sums = swap(send, "dp")
    layer_out, input_grad = call(
        last_kernel, [(ROWS, BF)] * 2, four, x, g, right_one, scratch=(WIDE_ROWS,)
    )
    (gr1,) = call(sum_kernel, [((4, 8, 128), F32)], sums)
    shape = (512, 4, 128)
    return (layer_out.reshape(shape), input_grad.reshape(shape), gr1, left[:4], gr2, left[4:])


def solution(mesh):
    placed = (
        P("dp", "tensor", None),
        P("tensor", None, None),
        P("tensor", None, None),
        P("tensor", None, None),
        P("tensor", None, None),
        P("dp", "tensor", None),
    )
    return jax.shard_map(
        on_device,
        mesh=mesh,
        in_specs=placed,
        out_specs=(
            P("dp", "tensor", None),
            P("dp", "tensor", None),
            P("tensor", "dp", None),
            P("tensor", "dp", None),
            P("tensor", "dp", None),
            P("tensor", "dp", None),
        ),
        check_vma=False,
    )
```

```python
import math

import jax
import jax.numpy as jnp
from jax import lax
from jax.experimental import pallas as pl
from jax.experimental.pallas import tpu as pltpu
from jax.sharding import PartitionSpec as P


BF = jnp.bfloat16
F32 = jnp.float32


def in_to_flat(r):
    return (r & 3) * 128 + (r >> 2)


def flat_to_in(r):
    return (r & 127) * 4 + (r >> 7)


def out_to_flat(r):
    return ((r >> 2) & 3) * 128 + (r >> 4) * 4 + (r & 3)


def flat_to_out(r):
    return ((r & 127) >> 2) * 16 + (r >> 7) * 4 + (r & 3)


def one_hot(col_of_row, cols=512):
    row = lax.broadcasted_iota(jnp.int32, (512, 128), 0)
    col = lax.broadcasted_iota(jnp.int32, (512, 128), 1)
    at = col_of_row(row)
    parts = [jnp.where(at == col + j, 1.0, 0.0).astype(BF) for j in range(0, cols, 128)]
    return jnp.concatenate(parts, axis=1)


def dot(a, b, dims):
    return lax.dot_general(a, b, (dims, ((), ())), preferred_element_type=F32)


def nn(a, b):
    return dot(a, b, ((1,), (0,)))


def nt(a, b):
    return dot(a, b, ((1,), (1,)))


def tn(a, b):
    return dot(a, b, ((0,), (0,)))


def put_rows(ref, first, value):
    ref[:, first : first + 16, :] = value.astype(BF).reshape(32, 16, 512)


def get_rows(ref, first):
    return ref[:, first : first + 16, :].reshape(512, 512)


def by_block(ref):
    return [ref[pl.ds(b, 512, stride=4), :].astype(BF) for b in range(4)]


def right_one_out(r1_ref):
    spread = one_hot(out_to_flat)
    cols = [nt(spread[:, 128 * b : 128 * b + 128], r1_ref[b]).astype(BF) for b in range(4)]
    return jnp.concatenate(cols, axis=1)


def fetch(pairs, sems):
    copies = [pltpu.make_async_copy(src, dst, sems.at[n]) for n, (src, dst) in enumerate(pairs)]
    for copy in copies:
        copy.start()
    return copies


def first_kernel(x_hbm, g_hbm, r1_hbm, out_ref, xs_ref, gs_ref, x_ref, g_ref, r1_ref, sems):
    r1_in, x_in, g_in = fetch(((r1_hbm, r1_ref), (x_hbm, x_ref), (g_hbm, g_ref)), sems)
    order = one_hot(in_to_flat)
    r1_in.wait()
    wide = right_one_out(r1_ref)
    x_in.wait()
    xs_ref[...] = x_ref[...].astype(F32)
    put_rows(out_ref, 0, nt(wide, jnp.concatenate(by_block(xs_ref), axis=1)))
    g_in.wait()
    gs_ref[...] = g_ref[...].astype(F32)
    put_rows(out_ref, 16, nt(order, jnp.concatenate(by_block(gs_ref), axis=1)))


def widen(w_ref, spread_in):
    parts = [nn(spread_in[:, 128 * b : 128 * b + 128], w_ref[b]).astype(BF) for b in range(4)]
    return jnp.concatenate(parts, axis=1)


def weights_kernel(fwd_ref, bwd_ref, fwd_out, bwd_out):
    spread_in = one_hot(in_to_flat)
    spread_out = one_hot(out_to_flat)
    fwd_out[...] = nt(spread_out, widen(fwd_ref, spread_in)).astype(BF)
    bwd_out[...] = nt(widen(bwd_ref, spread_in), spread_out).astype(BF)


def mix_kernel(got_ref, fwd_ref, bwd_ref, out_ref):
    put_rows(out_ref, 0, nn(fwd_ref[...], get_rows(got_ref, 0)))
    put_rows(out_ref, 16, nn(bwd_ref[...], get_rows(got_ref, 16)))


def gelu_kernel(got_ref, fwd_ref, bwd_ref, out_ref, h_ref):
    z = get_rows(got_ref, 0).astype(F32)
    cdf = 0.5 * (1.0 + lax.erf(z * (1.0 / math.sqrt(2.0))))
    h = (z * cdf).astype(BF)
    h_ref[...] = h
    put_rows(out_ref, 0, nn(fwd_ref[...], h))
    slope = cdf + z * jnp.exp(-0.5 * z * z) * (1.0 / math.sqrt(2.0 * math.pi))
    put_rows(out_ref, 16, nn(bwd_ref[...], get_rows(got_ref, 16)) * slope)


def grad_of(fwd, bwd, out_ref, first):
    a = nn(one_hot(flat_to_in), fwd).astype(BF)
    b = nn(one_hot(flat_to_out), bwd).astype(BF)
    for m in range(4):
        at = slice(128 * m, 128 * m + 128)
        out_ref[:, first + m, :, :] = nt(a[at], b[at]).reshape(16, 8, 128).astype(BF)


def hidden_grad_kernel(h_ref, got_hbm, out_ref, got_ref, sems):
    (got_in,) = fetch(((got_hbm, got_ref),), sems)
    got_in.wait()
    grad_of(h_ref[...], get_rows(got_ref, 16), out_ref, 0)


def left_grads_kernel(one_hbm, three_hbm, out_ref, one_ref, three_ref, sems):
    for copy in fetch(((one_hbm, one_ref), (three_hbm, three_ref)), sems):
        copy.wait()
    grad_of(get_rows(one_ref, 0), get_rows(three_ref, 16), out_ref, 0)
    grad_of(get_rows(three_ref, 0), get_rows(one_ref, 16), out_ref, 4)


def right_grad_kernel(got_ref, x_hbm, out_ref, xs_ref, x_ref, sems):
    (x_in,) = fetch(((x_hbm, x_ref),), sems)
    d = nn(one_hot(flat_to_out), get_rows(got_ref, 16)).astype(BF)
    x_in.wait()
    xs_ref[...] = x_ref[...].astype(F32)
    for b, x in enumerate(by_block(xs_ref)):
        g = jnp.transpose(nn(d[128 * b : 128 * b + 128], x))
        out_ref[:, b, :, :] = g.reshape(16, 8, 128).astype(BF)


def last_kernel(got_ref, x_ref, g_ref, r1_ref, out_ref, in_ref, s_ref):
    mixed = tn(get_rows(got_ref, 0), one_hot(in_to_flat))
    for b in range(4):
        s_ref[pl.ds(b, 512, stride=4), :] = mixed[:, 128 * b : 128 * b + 128]
    out_ref[...] = (x_ref[...].astype(F32) + s_ref[...]).astype(BF)
    back = tn(get_rows(got_ref, 16), right_one_out(r1_ref))
    for b in range(4):
        s_ref[pl.ds(b, 512, stride=4), :] = back[:, 128 * b : 128 * b + 128]
    in_ref[...] = (g_ref[...].astype(F32) + s_ref[...]).astype(BF)


def sum_kernel(got_ref, out_ref):
    total = got_ref[0].astype(F32)
    for k in range(1, 16):
        total = total + got_ref[k].astype(F32)
    out_ref[...] = total


ROWS = (2048, 128)
WIDE_ROWS = pltpu.VMEM(ROWS, F32)
HALF_ROWS = pltpu.VMEM(ROWS, BF)
CHUNK = pltpu.VMEM((32, 32, 512), BF)


def call(kernel, shapes, *args, scratch=(), far=()):
    args = [pltpu.with_memory_space_constraint(a, pltpu.HBM) if n in far else a for n, a in enumerate(args)]
    outs = [jax.ShapeDtypeStruct(s, d) for s, d in shapes]
    specs = [pl.BlockSpec(memory_space=pltpu.HBM if n in far else pltpu.VMEM) for n in range(len(args))]
    return pl.pallas_call(
        kernel,
        out_shape=outs,
        in_specs=specs,
        scratch_shapes=scratch,
        compiler_params=pltpu.CompilerParams(vmem_limit_bytes=16 << 20),
    )(*args)


def swap(x, axis):
    return lax.all_to_all(x, axis, 0, 0, tiled=True)


def sent(x, mask):
    return lax.ppermute(x, "dp", [(i, i ^ mask) for i in range(16)])


def added_near(parts):
    me = lax.axis_index("dp")
    rest = parts.shape[1:]
    parts = parts.reshape(2, 4, 2, *rest)

    def of(who):
        at = (who >> 3, 0, who & 1) + (0,) * len(rest)
        return lax.dynamic_slice(
            parts, at, (1, 4, 1, *rest), allow_negative_indices=False
        ).reshape(4, *rest)

    total = of(me).astype(F32)
    for mask in (8, 1, 9):
        total = total + sent(of(me ^ mask), mask).astype(F32)
    return total


def added_far(total):
    me = lax.axis_index("dp")

    def of(x, who):
        return lax.dynamic_index_in_dim(
            x, (who >> 1) & 3, 0, False, allow_negative_indices=False
        )

    half = total.astype(BF)
    own = of(total, me)
    for mask in (2, 4, 6):
        own = own + sent(of(half, me ^ mask), mask).astype(F32)
    return own


def after(first, *values):
    return lax.optimization_barrier((first, *values))[1:]


def on_device(tokens_in, right_one, left_one, right_two, left_two, out_grad):
    x = tokens_in.reshape(ROWS)
    g = out_grad.reshape(ROWS)
    chunk = ((32, 32, 512), BF)
    square = ((512, 512), BF)
    (send,) = call(
        first_kernel,
        [chunk],
        x,
        g,
        right_one,
        scratch=(
            WIDE_ROWS,
            WIDE_ROWS,
            HALF_ROWS,
            HALF_ROWS,
            pltpu.VMEM((4, 128, 128), BF),
            pltpu.SemaphoreType.DMA((3,)),
        ),
        far=(0, 1, 2),
    )
    one = swap(send, "tensor")
    fwd, bwd = call(weights_kernel, [square] * 2, *after(send, left_one, left_two))
    (send,) = call(mix_kernel, [chunk], one, fwd, bwd)
    (one,) = after(send, one)
    two = swap(send, "tensor")
    fwd, bwd = call(weights_kernel, [square] * 2, *after(send, right_two, right_two))
    send, h = call(gelu_kernel, [chunk, square], two, fwd, bwd)
    h, two = after(send, h, two)
    three = swap(send, "tensor")
    fwd, bwd = call(weights_kernel, [square] * 2, *after(send, left_two, left_one))
    (gr2,) = call(
        hidden_grad_kernel,
        [((16, 4, 8, 128), BF)],
        h,
        two,
        scratch=(CHUNK, pltpu.SemaphoreType.DMA((1,))),
        far=(1,),
    )
    gr2 = added_near(gr2)
    three, gr2 = lax.optimization_barrier((three, gr2))
    (send,) = call(mix_kernel, [chunk], three, fwd, bwd)
    (three,) = after(send, three)
    four = swap(send, "tensor")
    (left,) = call(
        left_grads_kernel,
        [((16, 8, 8, 128), BF)],
        one,
        three,
        scratch=(CHUNK, CHUNK, pltpu.SemaphoreType.DMA((2,))),
        far=(0, 1),
    )
    left = added_near(left)
    sums = added_far(jnp.concatenate((gr2, left), axis=1))
    four, sums = lax.optimization_barrier((four, sums))
    (send,) = call(
        right_grad_kernel,
        [((16, 4, 8, 128), BF)],
        four,
        x,
        scratch=(WIDE_ROWS, HALF_ROWS, pltpu.SemaphoreType.DMA((1,))),
        far=(1,),
    )
    got = swap(send, "dp")
    layer_out, input_grad = call(
        last_kernel, [(ROWS, BF)] * 2, four, x, g, right_one, scratch=(WIDE_ROWS,)
    )
    (gr1,) = call(sum_kernel, [((4, 8, 128), F32)], got)
    shape = (512, 4, 128)
    return (layer_out.reshape(shape), input_grad.reshape(shape), gr1, sums[4:8], sums[:4], sums[8:])


def solution(mesh):
    placed = (
        P("dp", "tensor", None),
        P("tensor", None, None),
        P("tensor", None, None),
        P("tensor", None, None),
        P("tensor", None, None),
        P("dp", "tensor", None),
    )
    return jax.shard_map(
        on_device,
        mesh=mesh,
        in_specs=placed,
        out_specs=(
            P("dp", "tensor", None),
            P("dp", "tensor", None),
            P("tensor", "dp", None),
            P("tensor", "dp", None),
            P("tensor", "dp", None),
            P("tensor", "dp", None),
        ),
        check_vma=False,
    )
```

```python
import math

import jax
import jax.numpy as jnp
from jax import lax
from jax.experimental import pallas as pl
from jax.experimental.pallas import tpu as pltpu
from jax.sharding import PartitionSpec as P


BF = jnp.bfloat16
F32 = jnp.float32


def in_to_flat(r):
    return (r & 3) * 128 + (r >> 2)


def flat_to_in(r):
    return (r & 127) * 4 + (r >> 7)


def out_to_flat(r):
    return ((r >> 2) & 3) * 128 + (r >> 4) * 4 + (r & 3)


def flat_to_out(r):
    return ((r & 127) >> 2) * 16 + (r >> 7) * 4 + (r & 3)


def one_hot(col_of_row, cols=512):
    row = lax.broadcasted_iota(jnp.int32, (512, 128), 0)
    col = lax.broadcasted_iota(jnp.int32, (512, 128), 1)
    at = col_of_row(row)
    parts = [jnp.where(at == col + j, 1.0, 0.0).astype(BF) for j in range(0, cols, 128)]
    return jnp.concatenate(parts, axis=1)


def dot(a, b, dims):
    return lax.dot_general(a, b, (dims, ((), ())), preferred_element_type=F32)


def nn(a, b):
    return dot(a, b, ((1,), (0,)))


def nt(a, b):
    return dot(a, b, ((1,), (1,)))


def tn(a, b):
    return dot(a, b, ((0,), (0,)))


def push(out_hbm, buf_ref, sems, first, rows_of):
    copies = []
    for half in range(2):
        at = (pl.ds(16 * half, 16), pl.ds(first, 16))
        value = rows_of(slice(256 * half, 256 * half + 256))
        buf_ref[at] = value.astype(BF).reshape(16, 16, 512)
        sem = sems.at[first // 8 + half]
        copies.append(pltpu.make_async_copy(buf_ref.at[at], out_hbm.at[at], sem))
        copies[-1].start()
    return copies


def finish(copies):
    for copy in copies:
        copy.wait()


def get_rows(ref, first):
    return ref[:, first : first + 16, :].reshape(512, 512)


def by_block(ref):
    return [ref[pl.ds(b, 512, stride=4), :].astype(BF) for b in range(4)]


def right_one_out(r1_ref):
    spread = one_hot(out_to_flat)
    cols = [nt(spread[:, 128 * b : 128 * b + 128], r1_ref[b]).astype(BF) for b in range(4)]
    return jnp.concatenate(cols, axis=1)


def fetch(pairs, sems):
    copies = [pltpu.make_async_copy(src, dst, sems.at[n]) for n, (src, dst) in enumerate(pairs)]
    for copy in copies:
        copy.start()
    return copies


def first_kernel(
    x_hbm, g_hbm, r1_hbm, out_hbm, xs_ref, gs_ref, x_ref, g_ref, r1_ref, sems, buf_ref, out_sems
):
    r1_in, x_in, g_in = fetch(((r1_hbm, r1_ref), (x_hbm, x_ref), (g_hbm, g_ref)), sems)
    order = one_hot(in_to_flat)
    r1_in.wait()
    wide = right_one_out(r1_ref)
    x_in.wait()
    xs_ref[...] = x_ref[...].astype(F32)
    x = jnp.concatenate(by_block(xs_ref), axis=1)
    fwd = push(out_hbm, buf_ref, out_sems, 0, lambda at: nt(wide[at], x))
    g_in.wait()
    gs_ref[...] = g_ref[...].astype(F32)
    g = jnp.concatenate(by_block(gs_ref), axis=1)
    finish(fwd + push(out_hbm, buf_ref, out_sems, 16, lambda at: nt(order[at], g)))


def widen(w_ref, spread_in):
    parts = [nn(spread_in[:, 128 * b : 128 * b + 128], w_ref[b]).astype(BF) for b in range(4)]
    return jnp.concatenate(parts, axis=1)


def weights_kernel(fwd_ref, bwd_ref, fwd_out, bwd_out):
    spread_in = one_hot(in_to_flat)
    spread_out = one_hot(out_to_flat)
    fwd_out[...] = nt(spread_out, widen(fwd_ref, spread_in)).astype(BF)
    bwd_out[...] = nt(widen(bwd_ref, spread_in), spread_out).astype(BF)


def mix_kernel(got_ref, fwd_ref, bwd_ref, out_hbm, buf_ref, sems):
    v = get_rows(got_ref, 0)
    fwd = push(out_hbm, buf_ref, sems, 0, lambda at: nn(fwd_ref[at], v))
    g = get_rows(got_ref, 16)
    finish(fwd + push(out_hbm, buf_ref, sems, 16, lambda at: nn(bwd_ref[at], g)))


def gelu_kernel(got_ref, fwd_ref, bwd_ref, out_hbm, h_ref, buf_ref, sems):
    z = get_rows(got_ref, 0).astype(F32)
    cdf = 0.5 * (1.0 + lax.erf(z * (1.0 / math.sqrt(2.0))))
    h = (z * cdf).astype(BF)
    h_ref[...] = h
    fwd = push(out_hbm, buf_ref, sems, 0, lambda at: nn(fwd_ref[at], h))
    slope = cdf + z * jnp.exp(-0.5 * z * z) * (1.0 / math.sqrt(2.0 * math.pi))
    g = get_rows(got_ref, 16)
    bwd = push(out_hbm, buf_ref, sems, 16, lambda at: nn(bwd_ref[at], g) * slope[at])
    finish(fwd + bwd)


def grad_of(fwd, bwd, out_ref, first):
    a = nn(one_hot(flat_to_in), fwd).astype(BF)
    b = nn(one_hot(flat_to_out), bwd).astype(BF)
    for m in range(4):
        at = slice(128 * m, 128 * m + 128)
        out_ref[:, first + m, :, :] = nt(a[at], b[at]).reshape(16, 8, 128).astype(BF)


def hidden_grad_kernel(h_ref, got_hbm, out_ref, got_ref, sems):
    (got_in,) = fetch(((got_hbm, got_ref),), sems)
    got_in.wait()
    grad_of(h_ref[...], get_rows(got_ref, 16), out_ref, 0)


def left_grads_kernel(one_hbm, three_hbm, out_ref, one_ref, three_ref, sems):
    for copy in fetch(((one_hbm, one_ref), (three_hbm, three_ref)), sems):
        copy.wait()
    grad_of(get_rows(one_ref, 0), get_rows(three_ref, 16), out_ref, 0)
    grad_of(get_rows(three_ref, 0), get_rows(one_ref, 16), out_ref, 4)


def turn_kernel(x_hbm, out_hbm, xs_ref, x_ref, xt_ref, sems):
    (x_in,) = fetch(((x_hbm, x_ref),), sems)
    x_in.wait()
    xs_ref[...] = x_ref[...].astype(F32)
    for b in range(4):
        xt_ref[b] = jnp.transpose(xs_ref[pl.ds(b, 512, stride=4), :]).astype(BF)
    out = pltpu.make_async_copy(xt_ref, out_hbm, sems.at[1])
    out.start()
    out.wait()


def right_grad_kernel(got_ref, xt_hbm, out_ref, xt_ref, sems):
    (xt_in,) = fetch(((xt_hbm, xt_ref),), sems)
    d = nn(one_hot(flat_to_out), get_rows(got_ref, 16)).astype(BF)
    xt_in.wait()
    for b in range(4):
        g = nt(xt_ref[b], d[128 * b : 128 * b + 128])
        out_ref[:, b, :, :] = g.reshape(16, 8, 128).astype(BF)


def last_kernel(got_ref, x_ref, g_ref, r1_ref, out_ref, in_ref, s_ref):
    mixed = tn(get_rows(got_ref, 0), one_hot(in_to_flat))
    for b in range(4):
        s_ref[pl.ds(b, 512, stride=4), :] = mixed[:, 128 * b : 128 * b + 128]
    out_ref[...] = (x_ref[...].astype(F32) + s_ref[...]).astype(BF)
    back = tn(get_rows(got_ref, 16), right_one_out(r1_ref))
    for b in range(4):
        s_ref[pl.ds(b, 512, stride=4), :] = back[:, 128 * b : 128 * b + 128]
    in_ref[...] = (g_ref[...].astype(F32) + s_ref[...]).astype(BF)


def sum_kernel(got_ref, out_ref):
    total = got_ref[0].astype(F32)
    for k in range(1, 16):
        total = total + got_ref[k].astype(F32)
    out_ref[...] = total


ROWS = (2048, 128)
WIDE_ROWS = pltpu.VMEM(ROWS, F32)
HALF_ROWS = pltpu.VMEM(ROWS, BF)
CHUNK = pltpu.VMEM((32, 32, 512), BF)
XT = pltpu.VMEM((4, 128, 512), BF)


def call(kernel, shapes, *args, scratch=(), far=(), far_out=()):
    args = [pltpu.with_memory_space_constraint(a, pltpu.HBM) if n in far else a for n, a in enumerate(args)]
    outs = [jax.ShapeDtypeStruct(s, d) for s, d in shapes]
    specs = [pl.BlockSpec(memory_space=pltpu.HBM if n in far else pltpu.VMEM) for n in range(len(args))]
    out_specs = [pl.BlockSpec(memory_space=pltpu.HBM if n in far_out else pltpu.VMEM) for n in range(len(outs))]
    return pl.pallas_call(
        kernel,
        out_shape=outs,
        out_specs=out_specs,
        in_specs=specs,
        scratch_shapes=scratch,
        compiler_params=pltpu.CompilerParams(vmem_limit_bytes=16 << 20),
    )(*args)


def swap(x, axis):
    return lax.all_to_all(x, axis, 0, 0, tiled=True)


def sent(x, mask):
    return lax.ppermute(x, "dp", [(i, i ^ mask) for i in range(16)])


def added_near(parts):
    me = lax.axis_index("dp")
    rest = parts.shape[1:]
    parts = parts.reshape(2, 4, 2, *rest)

    def of(who):
        at = (who >> 3, 0, who & 1) + (0,) * len(rest)
        return lax.dynamic_slice(
            parts, at, (1, 4, 1, *rest), allow_negative_indices=False
        ).reshape(4, *rest)

    total = of(me).astype(F32)
    for mask in (8, 1, 9):
        total = total + sent(of(me ^ mask), mask).astype(F32)
    return total


def added_far(total):
    me = lax.axis_index("dp")

    def of(x, who):
        return lax.dynamic_index_in_dim(
            x, (who >> 1) & 3, 0, False, allow_negative_indices=False
        )

    half = total.astype(BF)
    own = lax.optimization_barrier(of(total, me))
    for mask in (2, 4, 6):
        own = own + sent(of(half, me ^ mask), mask).astype(F32)
    return own


def after(first, *values):
    return lax.optimization_barrier((first, *values))[1:]


def on_device(tokens_in, right_one, left_one, right_two, left_two, out_grad):
    x = tokens_in.reshape(ROWS)
    g = out_grad.reshape(ROWS)
    chunk = ((32, 32, 512), BF)
    square = ((512, 512), BF)
    pushed = dict(scratch=(CHUNK, pltpu.SemaphoreType.DMA((4,))), far_out=(0,))
    (send,) = call(
        first_kernel,
        [chunk],
        x,
        g,
        right_one,
        scratch=(
            WIDE_ROWS,
            WIDE_ROWS,
            HALF_ROWS,
            HALF_ROWS,
            pltpu.VMEM((4, 128, 128), BF),
            pltpu.SemaphoreType.DMA((3,)),
            CHUNK,
            pltpu.SemaphoreType.DMA((4,)),
        ),
        far=(0, 1, 2),
        far_out=(0,),
    )
    one = swap(send, "tensor")
    fwd, bwd = call(weights_kernel, [square] * 2, *after(send, left_one, left_two))
    (send,) = call(mix_kernel, [chunk], one, fwd, bwd, **pushed)
    (one,) = after(send, one)
    two = swap(send, "tensor")
    fwd, bwd = call(weights_kernel, [square] * 2, *after(send, right_two, right_two))
    (xt,) = call(
        turn_kernel,
        [((4, 128, 512), BF)],
        *after(send, x),
        scratch=(WIDE_ROWS, HALF_ROWS, XT, pltpu.SemaphoreType.DMA((2,))),
        far=(0,),
        far_out=(0,),
    )
    two, xt = lax.optimization_barrier((two, xt))
    send, h = call(gelu_kernel, [chunk, square], two, fwd, bwd, **pushed)
    h, two = after(send, h, two)
    three = swap(send, "tensor")
    fwd, bwd = call(weights_kernel, [square] * 2, *after(send, left_two, left_one))
    (gr2,) = call(
        hidden_grad_kernel,
        [((16, 4, 8, 128), BF)],
        h,
        two,
        scratch=(CHUNK, pltpu.SemaphoreType.DMA((1,))),
        far=(1,),
    )
    gr2 = added_near(gr2)
    three, gr2 = lax.optimization_barrier((three, gr2))
    (send,) = call(mix_kernel, [chunk], three, fwd, bwd, **pushed)
    (three,) = after(send, three)
    four = swap(send, "tensor")
    (left,) = call(
        left_grads_kernel,
        [((16, 8, 8, 128), BF)],
        one,
        three,
        scratch=(CHUNK, CHUNK, pltpu.SemaphoreType.DMA((2,))),
        far=(0, 1),
    )
    left = added_near(left)
    sums = added_far(jnp.concatenate((gr2, left), axis=1))
    (send,) = call(
        right_grad_kernel,
        [((16, 4, 8, 128), BF)],
        four,
        xt,
        scratch=(XT, pltpu.SemaphoreType.DMA((1,))),
        far=(1,),
    )
    got = swap(send, "dp")
    layer_out, input_grad = call(
        last_kernel, [(ROWS, BF)] * 2, four, x, g, right_one, scratch=(WIDE_ROWS,)
    )
    (gr1,) = call(sum_kernel, [((4, 8, 128), F32)], got)
    shape = (512, 4, 128)
    return (layer_out.reshape(shape), input_grad.reshape(shape), gr1, sums[4:8], sums[:4], sums[8:])


def solution(mesh):
    placed = (
        P("dp", "tensor", None),
        P("tensor", None, None),
        P("tensor", None, None),
        P("tensor", None, None),
        P("tensor", None, None),
        P("dp", "tensor", None),
    )
    return jax.shard_map(
        on_device,
        mesh=mesh,
        in_specs=placed,
        out_specs=(
            P("dp", "tensor", None),
            P("dp", "tensor", None),
            P("tensor", "dp", None),
            P("tensor", "dp", None),
            P("tensor", "dp", None),
            P("tensor", "dp", None),
        ),
        check_vma=False,
    )
```

```python
import functools
import math

import jax
import jax.numpy as jnp
from jax import lax
from jax.experimental import pallas as pl
from jax.experimental.pallas import tpu as pltpu
from jax.sharding import Mesh
from jax.sharding import PartitionSpec as P


BF = jnp.bfloat16
F32 = jnp.float32


def in_to_flat(r):
    return (r & 3) * 128 + (r >> 2)


def flat_to_in(r):
    return (r & 127) * 4 + (r >> 7)


def out_to_flat(r):
    return ((r >> 2) & 3) * 128 + (r >> 4) * 4 + (r & 3)


def flat_to_out(r):
    return ((r & 127) >> 2) * 16 + (r >> 7) * 4 + (r & 3)


def one_hot(col_of_row, cols=512):
    row = lax.broadcasted_iota(jnp.int32, (512, 128), 0)
    col = lax.broadcasted_iota(jnp.int32, (512, 128), 1)
    at = col_of_row(row)
    parts = [jnp.where(at == col + j, 1.0, 0.0).astype(BF) for j in range(0, cols, 128)]
    return jnp.concatenate(parts, axis=1)


def dot(a, b, dims):
    return lax.dot_general(a, b, (dims, ((), ())), preferred_element_type=F32)


def nn(a, b):
    return dot(a, b, ((1,), (0,)))


def nt(a, b):
    return dot(a, b, ((1,), (1,)))


def tn(a, b):
    return dot(a, b, ((0,), (0,)))


def push(out_hbm, buf_ref, sems, first, rows_of):
    copies = []
    for half in range(2):
        at = (pl.ds(16 * half, 16), pl.ds(first, 16))
        value = rows_of(slice(256 * half, 256 * half + 256))
        buf_ref[at] = value.astype(BF).reshape(16, 16, 512)
        sem = sems.at[first // 8 + half]
        copies.append(pltpu.make_async_copy(buf_ref.at[at], out_hbm.at[at], sem))
        copies[-1].start()
    return copies


def push_wide(out_hbm, buf_ref, sems, first, rows_of, lanes_first):
    copies = []
    for half in range(2):
        value = rows_of(slice(256 * half, 256 * half + 256)).astype(BF)
        for q in (2 * half, 2 * half + 1):
            rows = value[128 * (q & 1) : 128 * (q & 1) + 128].reshape(8, 16, 512)
            for w in range(4):
                part = rows[:, :, 128 * w : 128 * w + 128]
                at = (w, q) if lanes_first else (q, w)
                buf_ref[(*at, slice(None), pl.ds(first, 16), slice(None))] = part
        two = pl.ds(2 * half, 2)
        at = (slice(None), two) if lanes_first else (two, slice(None))
        at = (*at, slice(None), pl.ds(first, 16))
        sem = sems.at[first // 8 + half]
        copies.append(pltpu.make_async_copy(buf_ref.at[at], out_hbm.at[at], sem))
        copies[-1].start()
    return copies


def finish(copies):
    for copy in copies:
        copy.wait()


def get_rows(ref, first):
    return ref[:, first : first + 16, :].reshape(512, 512)


def get_by_first(ref, first):
    parts = [ref[w, :, :, first : first + 16, :].reshape(512, 128) for w in range(4)]
    return jnp.concatenate(parts, axis=1)


def get_by_second(ref, first):
    parts = [ref[:, w, :, first : first + 16, :].reshape(512, 128) for w in range(4)]
    return jnp.concatenate(parts, axis=1)


def by_block(ref):
    return [ref[pl.ds(b, 512, stride=4), :].astype(BF) for b in range(4)]


def right_one_out(r1_ref):
    spread = one_hot(out_to_flat)
    cols = [nt(spread[:, 128 * b : 128 * b + 128], r1_ref[b]).astype(BF) for b in range(4)]
    return jnp.concatenate(cols, axis=1)


def fetch(pairs, sems):
    copies = [pltpu.make_async_copy(src, dst, sems.at[n]) for n, (src, dst) in enumerate(pairs)]
    for copy in copies:
        copy.start()
    return copies


def first_kernel(
    x_hbm, g_hbm, r1_hbm, out_hbm, xs_ref, gs_ref, x_ref, g_ref, r1_ref, sems, buf_ref, out_sems
):
    r1_in, x_in, g_in = fetch(((r1_hbm, r1_ref), (x_hbm, x_ref), (g_hbm, g_ref)), sems)
    order = one_hot(in_to_flat)
    r1_in.wait()
    wide = right_one_out(r1_ref)
    x_in.wait()
    xs_ref[...] = x_ref[...].astype(F32)
    x = jnp.concatenate(by_block(xs_ref), axis=1)
    fwd = push_wide(out_hbm, buf_ref, out_sems, 0, lambda at: nt(wide[at], x), False)
    g_in.wait()
    gs_ref[...] = g_ref[...].astype(F32)
    g = jnp.concatenate(by_block(gs_ref), axis=1)
    bwd = push_wide(out_hbm, buf_ref, out_sems, 16, lambda at: nt(order[at], g), False)
    finish(fwd + bwd)


def widen(w_ref, n, spread_in):
    parts = [nn(spread_in[:, 128 * b : 128 * b + 128], w_ref[n, b]).astype(BF) for b in range(4)]
    return jnp.concatenate(parts, axis=1)


def weights_kernel(n_fwd, n_bwd, w_ref, fwd_out, bwd_out):
    spread_in = one_hot(in_to_flat)
    spread_out = one_hot(out_to_flat)
    fwd_out[...] = nt(spread_out, widen(w_ref, n_fwd, spread_in)).astype(BF)
    bwd_out[...] = nt(widen(w_ref, n_bwd, spread_in), spread_out).astype(BF)


def mix_kernel(got_ref, fwd_ref, bwd_ref, out_hbm, buf_ref, sems):
    v = get_by_first(got_ref, 0)
    fwd = push(out_hbm, buf_ref, sems, 0, lambda at: nn(fwd_ref[at], v))
    g = get_by_first(got_ref, 16)
    finish(fwd + push(out_hbm, buf_ref, sems, 16, lambda at: nn(bwd_ref[at], g)))


def mix_back_kernel(got_ref, fwd_ref, bwd_ref, out_hbm, buf_ref, sems):
    v = get_rows(got_ref, 0)
    fwd = push_wide(out_hbm, buf_ref, sems, 0, lambda at: nn(fwd_ref[at], v), True)
    g = get_rows(got_ref, 16)
    finish(fwd + push_wide(out_hbm, buf_ref, sems, 16, lambda at: nn(bwd_ref[at], g), True))


def gelu_kernel(got_ref, fwd_ref, bwd_ref, out_hbm, h_ref, buf_ref, sems):
    z = get_rows(got_ref, 0).astype(F32)
    cdf = 0.5 * (1.0 + lax.erf(z * (1.0 / math.sqrt(2.0))))
    h = (z * cdf).astype(BF)
    h_ref[...] = h
    fwd = push(out_hbm, buf_ref, sems, 0, lambda at: nn(fwd_ref[at], h))
    slope = cdf + z * jnp.exp(-0.5 * z * z) * (1.0 / math.sqrt(2.0 * math.pi))
    g = get_rows(got_ref, 16)
    bwd = push(out_hbm, buf_ref, sems, 16, lambda at: nn(bwd_ref[at], g) * slope[at])
    finish(fwd + bwd)


def grad_of(fwd, bwd, out_ref, first):
    a = nn(one_hot(flat_to_in), fwd).astype(BF)
    b = nn(one_hot(flat_to_out), bwd).astype(BF)
    for m in range(4):
        at = slice(128 * m, 128 * m + 128)
        out_ref[:, first + m, :, :] = nt(a[at], b[at]).reshape(16, 8, 128).astype(BF)


def hidden_grad_kernel(h_ref, got_hbm, out_ref, got_ref, sems):
    (got_in,) = fetch(((got_hbm, got_ref),), sems)
    got_in.wait()
    grad_of(h_ref[...], get_rows(got_ref, 16), out_ref, 0)


def left_grads_kernel(one_hbm, three_hbm, out_ref, one_ref, three_ref, sems):
    for copy in fetch(((one_hbm, one_ref), (three_hbm, three_ref)), sems):
        copy.wait()
    grad_of(get_by_first(one_ref, 0), get_rows(three_ref, 16), out_ref, 0)
    grad_of(get_rows(three_ref, 0), get_by_first(one_ref, 16), out_ref, 4)


def turn_kernel(x_hbm, out_hbm, xs_ref, x_ref, xt_ref, sems):
    (x_in,) = fetch(((x_hbm, x_ref),), sems)
    x_in.wait()
    xs_ref[...] = x_ref[...].astype(F32)
    for b in range(4):
        xt_ref[b] = jnp.transpose(xs_ref[pl.ds(b, 512, stride=4), :]).astype(BF)
    out = pltpu.make_async_copy(xt_ref, out_hbm, sems.at[1])
    out.start()
    out.wait()


def right_grad_kernel(got_ref, xt_hbm, out_ref, xt_ref, sems):
    (xt_in,) = fetch(((xt_hbm, xt_ref),), sems)
    d = nn(one_hot(flat_to_out), get_by_second(got_ref, 16)).astype(BF)
    xt_in.wait()
    for b in range(4):
        g = nt(xt_ref[b], d[128 * b : 128 * b + 128])
        out_ref[:, b, :, :] = g.reshape(16, 8, 128).astype(BF)


def last_kernel(got_ref, x_ref, g_ref, r1_ref, out_ref, in_ref, s_ref):
    mixed = tn(get_by_second(got_ref, 0), one_hot(in_to_flat))
    for b in range(4):
        s_ref[pl.ds(b, 512, stride=4), :] = mixed[:, 128 * b : 128 * b + 128]
    out_ref[...] = (x_ref[...].astype(F32) + s_ref[...]).astype(BF)
    back = tn(get_by_second(got_ref, 16), right_one_out(r1_ref))
    for b in range(4):
        s_ref[pl.ds(b, 512, stride=4), :] = back[:, 128 * b : 128 * b + 128]
    in_ref[...] = (g_ref[...].astype(F32) + s_ref[...]).astype(BF)


def sum_kernel(got_ref, out_ref):
    total = got_ref[0].astype(F32)
    for k in range(1, 16):
        total = total + got_ref[k].astype(F32)
    out_ref[...] = total


ROWS = (2048, 128)
WIDE_ROWS = pltpu.VMEM(ROWS, F32)
HALF_ROWS = pltpu.VMEM(ROWS, BF)
CHUNK = pltpu.VMEM((32, 32, 512), BF)
WIDE_CHUNK = pltpu.VMEM((4, 4, 8, 32, 128), BF)
XT = pltpu.VMEM((4, 128, 512), BF)


def call(kernel, shapes, *args, scratch=(), far=(), far_out=(), static=()):
    args = [pltpu.with_memory_space_constraint(a, pltpu.HBM) if n in far else a for n, a in enumerate(args)]
    outs = [jax.ShapeDtypeStruct(s, d) for s, d in shapes]
    specs = [pl.BlockSpec(memory_space=pltpu.HBM if n in far else pltpu.VMEM) for n in range(len(args))]
    out_specs = [pl.BlockSpec(memory_space=pltpu.HBM if n in far_out else pltpu.VMEM) for n in range(len(outs))]
    return pl.pallas_call(
        functools.partial(kernel, *static),
        out_shape=outs,
        out_specs=out_specs,
        in_specs=specs,
        scratch_shapes=scratch,
        compiler_params=pltpu.CompilerParams(vmem_limit_bytes=16 << 20),
    )(*args)


DP = ("xlo", "yhi", "ylo")
TENSOR = ("zhi", "zlo", "xhi", "core")
OUTER = ("ylo", "xlo", "zhi", "zlo", "xhi", "core")
INNER = ("ylo", "xlo", "zlo", "xhi", "core")


def swap(x, axis):
    return lax.all_to_all(x, axis, 0, 0, tiled=True)


def outer_swap(x):
    return swap(x.reshape(128, 32, 128), OUTER).reshape(4, 4, 8, 32, 128)


def turned(x):
    flip = (0, 2, 1, 3)
    pairs = [(4 * flip[a] + b, 4 * flip[b] + a) for a in range(4) for b in range(4)]
    return lax.ppermute(x, ("xlo", "ylo", "zhi"), pairs)


def moved_factors(factors):
    me = lax.axis_index("yhi")
    rows = [
        lax.dynamic_slice(f, (0, 32 * me, 0), (4, 32, 128), allow_negative_indices=False)
        for f in factors
    ]
    mine = turned(jnp.stack(rows))
    every = jnp.zeros((3, 4, 4, 32, 128), BF)
    for mask in range(4):
        piece = sent(mine, "yhi", mask) if mask else mine
        at = (0, 0, me ^ mask, 0, 0)
        every = lax.dynamic_update_slice(every, piece[:, :, None], at, allow_negative_indices=False)
    return every.reshape(3, 4, 128, 128)


def sent(x, axis, mask):
    return lax.ppermute(x, axis, [(i, i ^ mask) for i in range(4)])


def added_near(parts):
    me = lax.axis_index("yhi")
    rest = parts.shape[1:]
    parts = parts.reshape(2, 4, 2, *rest)

    def of(who):
        at = (0, who, 0) + (0,) * len(rest)
        return lax.dynamic_slice(
            parts, at, (2, 1, 2, *rest), allow_negative_indices=False
        ).reshape(2, 2, *rest)

    total = of(me).astype(F32)
    for mask in (1, 2, 3):
        total = total + sent(of(me ^ mask), "yhi", mask).astype(F32)
    return total


def added_far(total):
    me = lax.axis_index("zhi")
    rest = total.shape[2:]

    def of(x, who):
        at = (who & 1, who >> 1) + (0,) * len(rest)
        return lax.dynamic_slice(x, at, (1, 1, *rest), allow_negative_indices=False).reshape(rest)

    half = total.astype(BF)
    own = lax.optimization_barrier(of(total, me))
    for mask in (1, 2, 3):
        own = own + sent(of(half, me ^ mask), "zhi", mask).astype(F32)
    return own


def after(first, *values):
    return lax.optimization_barrier((first, *values))[1:]


def on_device(tokens_in, right_one, left_one, right_two, left_two, out_grad):
    x = tokens_in.reshape(ROWS)
    g = out_grad.reshape(ROWS)
    chunk = ((32, 32, 512), BF)
    wide_chunk = ((4, 4, 8, 32, 128), BF)
    square = ((512, 512), BF)
    pushed = dict(scratch=(CHUNK, pltpu.SemaphoreType.DMA((4,))), far_out=(0,))
    pushed_wide = dict(scratch=(WIDE_CHUNK, pltpu.SemaphoreType.DMA((4,))), far_out=(0,))
    (send,) = call(
        first_kernel,
        [wide_chunk],
        x,
        g,
        right_one,
        scratch=(
            WIDE_ROWS,
            WIDE_ROWS,
            HALF_ROWS,
            HALF_ROWS,
            pltpu.VMEM((4, 128, 128), BF),
            pltpu.SemaphoreType.DMA((3,)),
            WIDE_CHUNK,
            pltpu.SemaphoreType.DMA((4,)),
        ),
        far=(0, 1, 2),
        far_out=(0,),
    )
    one = outer_swap(send)
    factors = moved_factors((left_one, right_two, left_two))
    l1, r2, l2 = range(3)
    fwd, bwd = call(weights_kernel, [square] * 2, factors, static=(l1, l2))
    (send,) = call(mix_kernel, [chunk], one, fwd, bwd, **pushed)
    (one,) = after(send, one)
    two = swap(send, INNER)
    fwd, bwd = call(weights_kernel, [square] * 2, *after(send, factors), static=(r2, r2))
    (xt,) = call(
        turn_kernel,
        [((4, 128, 512), BF)],
        *after(send, x),
        scratch=(WIDE_ROWS, HALF_ROWS, XT, pltpu.SemaphoreType.DMA((2,))),
        far=(0,),
        far_out=(0,),
    )
    two, xt = lax.optimization_barrier((two, xt))
    send, h = call(gelu_kernel, [chunk, square], two, fwd, bwd, **pushed)
    h, two = after(send, h, two)
    three = swap(send, INNER)
    fwd, bwd = call(weights_kernel, [square] * 2, *after(send, factors), static=(l2, l1))
    (gr2,) = call(
        hidden_grad_kernel,
        [((16, 4, 8, 128), BF)],
        h,
        two,
        scratch=(CHUNK, pltpu.SemaphoreType.DMA((1,))),
        far=(1,),
    )
    gr2 = added_near(gr2)
    (send,) = call(mix_back_kernel, [wide_chunk], three, fwd, bwd, **pushed_wide)
    (three,) = after(send, three)
    four = outer_swap(send)
    (left,) = call(
        left_grads_kernel,
        [((16, 8, 8, 128), BF)],
        one,
        three,
        scratch=(WIDE_CHUNK, CHUNK, pltpu.SemaphoreType.DMA((2,))),
        far=(0, 1),
    )
    left = added_near(left)
    sums = turned(added_far(jnp.concatenate((gr2, left), axis=2)))
    (send,) = call(
        right_grad_kernel,
        [((16, 4, 8, 128), BF)],
        four,
        xt,
        scratch=(XT, pltpu.SemaphoreType.DMA((1,))),
        far=(1,),
    )
    got = swap(send, DP)
    layer_out, input_grad = call(
        last_kernel, [(ROWS, BF)] * 2, four, x, g, right_one, scratch=(WIDE_ROWS,)
    )
    (gr1,) = call(sum_kernel, [((4, 8, 128), F32)], got)
    shape = (512, 4, 128)
    return (layer_out.reshape(shape), input_grad.reshape(shape), gr1, sums[4:8], sums[:4], sums[8:])


def solution(mesh):
    sizes = (2, 4, 2, 4, 2, 2, 2)
    split = Mesh(mesh.devices.reshape(sizes), (*DP, *TENSOR))
    placed = (
        P(DP, TENSOR, None),
        P(TENSOR, None, None),
        P(TENSOR, None, None),
        P(TENSOR, None, None),
        P(TENSOR, None, None),
        P(DP, TENSOR, None),
    )
    return jax.shard_map(
        on_device,
        mesh=split,
        in_specs=placed,
        out_specs=(
            P(DP, TENSOR, None),
            P(DP, TENSOR, None),
            P(TENSOR, DP, None),
            P(TENSOR, DP, None),
            P(TENSOR, DP, None),
            P(TENSOR, DP, None),
        ),
        check_vma=False,
    )
```
